256 devices in a mesh: dp: 32 (over x_hi, z, core), mp: 8 (over x_lo, y).
Axes of the slice: x: 4 (x_hi: 2, x_lo: 2; x = x_hi * 2 + x_lo), y: 4, z: 8, core: 2. Of those that a mesh axis runs over, the one named last changes fastest.
Arguments:
- context: bfloat16 [8192, 6144], P('dp', 'mp'), may hold values from -6 to 6
- out_grad: bfloat16 [8192, 6144], P('dp', 'mp'), may hold values from -1.0546875 to 1.0546875
- master: float32 [8, 36864, 128], P('mp', 'dp'), may hold values from -0.078125 to 0.078125
- moment_one: float32 [8, 36864, 128], P('mp', 'dp'), may hold values from -3 to 3
- moment_two: float32 [8, 36864, 128], P('mp', 'dp'), may hold values from 1 to 64
- new_owner: int32 [32], replicated, may hold values from 0 to 31, as said below
- old_pieces: int32 [32, 32, 36], replicated, may hold values from 0 to 36863, as said below
Outputs:
- proj_out: bfloat16 [8192, 6144], P('dp', 'mp')
- master_out: float32 [8, 36864, 128], P('mp', 'dp')
- moment_one_out: float32 [8, 36864, 128], P('mp', 'dp')
- moment_two_out: float32 [8, 36864, 128], P('mp', 'dp')
The draws below stay inside these ranges and needn't reach their ends.
Inputs may be any that keep to these rules, and one draw needn't show every extreme that they name: `new_owner`: each index of dp appears exactly once. Every block number appears exactly once; old_pieces[i, j, :] lie from new_owner[j] * 1152 to new_owner[j] * 1152 + 1151.
All inputs are finite; a program needn't handle non-finite values.
Results may differ from the reference program's by a relative error of at most 0.015.
Values may be sent and summed in bfloat16 or wider, within the bound.
No kernel may reach another device: no remote copies, remote signals or barrier semaphores. Data moves between devices by JAX's collectives and lax.ppermute only.
A program may use at most 64 MiB of HBM per device.

```python
import math
import jax
import jax.numpy as jnp
from jax import lax

HEADS = 48
HD = 128
DW = 6144
BW = 128
TOK_DEV = 256
TOKENS = 8192
BLOCKS_DEV = 1152
PIECES = 36
N_DP = 32
N_MP = 8


def shard_maps(key):
    owner_key = jax.random.fold_in(key, 11)
    piece_key = jax.random.fold_in(key, 12)
    owners = jax.random.permutation(owner_key, N_DP).astype(jnp.int32)
    row_keys = jax.random.split(piece_key, N_DP)

    def shuffle_one(row_key):
        return jax.random.permutation(row_key, BLOCKS_DEV)
    shuffles = jax.vmap(shuffle_one)(row_keys).astype(jnp.int32)
    blocks_all = owners[:, None] * BLOCKS_DEV + shuffles
    arranged = blocks_all.reshape(N_DP, N_DP, PIECES).transpose(1, 0, 2)
    return (owners, arranged.astype(jnp.int32))


def draw_new_owner(key, part):
    return shard_maps(key)[0]


def draw_old_pieces(key, part):
    return shard_maps(key)[1]


def with_spikes(array, key, source, target, parts, factor):
    def block_of(dim):
        return (jnp.arange(array.shape[dim]) // (array.shape[dim] // parts)).reshape((-1,) + (1,) * (array.ndim - 1 - dim))

    one_side = jax.random.permutation(key, parts)[block_of(target)]
    other_side = (block_of(target) + parts // 2) % parts
    return jnp.where((block_of(source) == one_side) | (block_of(source) == other_side), factor * array, array)


def levels(key, extent, pieces, smallest, high):
    level, own = 1.0, jax.random.fold_in(key, 6)
    for position, shards_of in pieces:
        draws = jnp.exp(jax.random.uniform(jax.random.fold_in(own, position), (shards_of,), jnp.float32, smallest / len(pieces), high / len(pieces)))
        level = level * jnp.repeat(draws, extent[position] // shards_of).reshape([-1 if axis == position else 1 for axis in range(len(extent))])
    return level


def normal_values(own_key, extent, width, most, cuts=(), kind=jnp.bfloat16):
    values = width * jax.random.normal(own_key, extent, jnp.float32)
    if cuts:
        values = values * levels(own_key, extent, cuts, -0.22, 0.18)
    return jnp.clip(values, -most, most).astype(kind)


def noise_with(key, dims, width, most, cuts, heavy, kind=jnp.bfloat16):
    drawn = width * jax.random.normal(key, dims, jnp.float32)
    if cuts:
        drawn = drawn * levels(key, dims, cuts, -0.22, 0.18)
    return jnp.clip(with_spikes(drawn, jax.random.fold_in(key, 3), *heavy), -most, most).astype(kind)


def setup_inputs(seed: int = 0) -> dict:
    key_of = jax.random.split(jax.random.key(seed), 8)
    context = noise_with(key_of[0], (TOKENS, HEADS * HD), 1.0, 6.0, ((0, 32), (1, 8)), (0, 1, 32, 2.75))
    out_grad = normal_values(key_of[1], (TOKENS, DW), (16.0 * TOKENS ** -0.5), 1.0546875, ((0, 32), (1, 8)))
    master = normal_values(key_of[2], (N_MP, N_DP * BLOCKS_DEV, BW), (HEADS * HD) ** -0.5, 0.078125, ((0, 8), (1, 32)), jnp.float32)
    moment_one = normal_values(key_of[3], (N_MP, N_DP * BLOCKS_DEV, BW), 0.5, 3.0, ((0, 8), (1, 32)), jnp.float32)
    moment_two = jnp.clip(jnp.exp(math.log(64.0) - 4.158883 * jax.random.uniform(key_of[4], (N_MP, N_DP * BLOCKS_DEV, BW), jnp.float32) ** levels(key_of[4], (N_MP, N_DP * BLOCKS_DEV, BW), ((0, 8), (1, 32)), -0.2, 0.2)), 1.0, 64.0)
    new_owner = draw_new_owner(jax.random.fold_in(key_of[7], 71), 0)
    old_pieces = draw_old_pieces(jax.random.fold_in(key_of[7], 71), 0)
    return dict(context=context, out_grad=out_grad, master=master, moment_one=moment_one, moment_two=moment_two, new_owner=new_owner, old_pieces=old_pieces)


beta_one = 0.9
beta_two = 0.999
learn_rate = 0.001
decay_rate = 0.1
epsilon = 1e-08
step_count = 100.0

def adamw(weights, first_moment, second_moment, gradient):
    first_new = beta_one * first_moment + (1.0 - beta_one) * gradient
    second_new = beta_two * second_moment + (1.0 - beta_two) * gradient * gradient
    corrected_first = first_new / (1.0 - beta_one ** step_count)
    corrected_second = second_new / (1.0 - beta_two ** step_count)
    update = corrected_first / (jnp.sqrt(corrected_second) + epsilon)
    weights_new = weights - learn_rate * (update + decay_rate * weights)
    return (weights_new, first_new, second_new)

def reference(context, out_grad, master, moment_one, moment_two, new_owner, old_pieces):
    every_block = old_pieces.reshape(-1).astype(jnp.int32)

    def canonical(state_array):
        return jnp.zeros(state_array.shape, state_array.dtype).at[:, every_block].set(state_array)
    weights = canonical(master)
    first_moment = canonical(moment_one)
    second_moment = canonical(moment_two)
    matrix = weights.reshape(HEADS * HD, DW).astype(jnp.bfloat16)
    proj_out = jnp.dot(context, matrix, preferred_element_type=jnp.float32).astype(jnp.bfloat16)

    def accumulate(index, running_sum):
        first_row = (index * TOK_DEV).astype(jnp.int32)
        token_rows = lax.dynamic_slice_in_dim(context, first_row, TOK_DEV, 0)
        grad_rows = lax.dynamic_slice_in_dim(out_grad, first_row, TOK_DEV, 0)
        partial_sum = jnp.dot(token_rows.T, grad_rows, preferred_element_type=jnp.float32)
        rounded = lax.optimization_barrier(partial_sum.astype(jnp.bfloat16))
        return running_sum + rounded.astype(jnp.float32)
    gradient = lax.fori_loop(0, N_DP, accumulate, jnp.zeros((HEADS * HD, DW), jnp.float32))
    gradient = gradient.reshape(N_MP, N_DP * BLOCKS_DEV, BW)
    weights_new, first_new, second_new = adamw(weights, first_moment, second_moment, gradient)

    def relaid(state_array):
        grouped = state_array.reshape(N_MP, N_DP, BLOCKS_DEV, BW)
        return grouped[:, new_owner.astype(jnp.int32)].reshape(N_MP, N_DP * BLOCKS_DEV, BW)
    return (proj_out, relaid(weights_new), relaid(first_new), relaid(second_new))
```

```python
import jax
import jax.numpy as jnp
from jax import lax
from jax.sharding import Mesh, PartitionSpec as P

beta_one = 0.9
beta_two = 0.999
learn_rate = 0.001
decay_rate = 0.1
epsilon = 1e-08
step_count = 100.0

DP = ("xh", "z", "c")
MP = ("xl", "y")
DL = ("xh", "c")


def adamw(weights, first_moment, second_moment, gradient):
    first_new = beta_one * first_moment + (1.0 - beta_one) * gradient
    second_new = beta_two * second_moment + (1.0 - beta_two) * gradient * gradient
    corrected_first = first_new / (1.0 - beta_one**step_count)
    corrected_second = second_new / (1.0 - beta_two**step_count)
    update = corrected_first / (jnp.sqrt(corrected_second) + epsilon)
    weights_new = weights - learn_rate * (update + decay_rate * weights)
    return (weights_new, first_new, second_new)


def one_hot(index, count):
    rows = lax.broadcasted_iota(jnp.int32, (count, index.shape[0]), 0)
    return (rows == index[None, :]).astype(jnp.bfloat16)


def local(context, out_grad, master, moment_one, moment_two, new_owner, old_pieces):
    f32, bf16 = jnp.float32, jnp.bfloat16
    n_dp, n_mp = lax.axis_size(DP), lax.axis_size(MP)
    n_z, n_dl = lax.axis_size("z"), lax.axis_size(DL)
    n_xh, n_c = lax.axis_size("xh"), lax.axis_size("c")
    d = lax.axis_index(DP)
    blocks, width = master.shape[1:]
    tokens, cols = context.shape
    per_dev = cols // width
    per_row = per_dev * n_mp
    rows = blocks // per_row
    own_slab = new_owner[d]
    positions = (lax.dynamic_index_in_dim(old_pieces, d, 1, keepdims=False) - own_slab * blocks).reshape(-1)

    w_in = lax.all_to_all(master[0].astype(bf16), DP, 0, 0, tiled=True)
    moments = jnp.concatenate([moment_one[0], moment_two[0]], axis=1).astype(bf16)
    m_in = lax.all_to_all(moments, DP, 0, 0, tiled=True)

    owner_order = new_owner.reshape(n_xh, n_z, n_c).transpose(0, 2, 1).reshape(-1)
    wanted = (owner_order[:, None] * rows + jnp.arange(rows, dtype=jnp.int32)[None]).reshape(-1)
    columns = lax.broadcasted_iota(jnp.int32, (cols, cols), 1)
    select = (columns == wanted[:, None]).astype(bf16)
    ct = lax.dot_general(select, context, (((1,), (1,)), ((), ())), preferred_element_type=f32).astype(bf16)
    ct = lax.all_to_all(ct.reshape(n_dl, n_z * rows, tokens), DL, 0, 0, tiled=True)
    ct = lax.all_gather(ct, MP, axis=0, tiled=False)
    ct = ct.reshape(n_mp, n_dl, n_z, rows, tokens).transpose(0, 2, 3, 1, 4).reshape(n_mp * n_z * rows, n_dl * tokens)
    og = lax.all_gather(out_grad, DL, axis=0, tiled=True)

    grad = jnp.dot(ct, og, preferred_element_type=f32).astype(bf16)
    grad = lax.psum_scatter(grad.reshape(n_mp, n_z, rows, cols), "z", scatter_dimension=1, tiled=True)
    grad = lax.all_to_all(grad.reshape(n_mp, rows, cols), MP, 0, 0, tiled=True)
    grad = grad.reshape(n_mp, rows, per_dev, width).transpose(1, 0, 2, 3).reshape(blocks, width).astype(f32)

    w_at = (positions % per_row) * rows + positions // per_row
    w_t = jnp.dot(one_hot(w_at, blocks), w_in, preferred_element_type=f32).astype(bf16)
    w_t = lax.all_to_all(w_t.reshape(n_mp, per_dev, rows, width), MP, 0, 0, tiled=True)
    w_t = lax.all_gather(w_t, "z", axis=0, tiled=False)
    w_t = w_t.transpose(1, 0, 3, 2, 4).reshape(n_mp * n_z * rows, cols)
    out = lax.dot_general(ct, w_t, (((0,), (0,)), ((), ())), preferred_element_type=f32).astype(bf16)
    proj_out = lax.psum_scatter(out, DL, scatter_dimension=0, tiled=True)

    placed = jnp.dot(
        one_hot(positions, blocks), jnp.concatenate([w_in, m_in], axis=1), preferred_element_type=f32
    )
    weights, first_moment, second_moment = (placed[:, i * width : (i + 1) * width] for i in range(3))
    weights_new, first_new, second_new = adamw(weights, first_moment, second_moment, grad)
    return (proj_out, weights_new[None], first_new[None], second_new[None])


def solution(mesh):
    fine = Mesh(mesh.devices.reshape(2, 8, 2, 2, 4), DP[:2] + ("c",) + MP)
    placed = (P(DP, MP), P(DP, MP), P(MP, DP, None), P(MP, DP, None), P(MP, DP, None), P(), P())
    return jax.shard_map(
        local,
        mesh=fine,
        in_specs=placed,
        out_specs=(P(DP, MP), P(MP, DP, None), P(MP, DP, None), P(MP, DP, None)),
        check_vma=False,
    )
```

```python
import jax
import jax.numpy as jnp
from jax import lax
from jax.experimental import pallas as pl
from jax.experimental.pallas import tpu as pltpu
from jax.sharding import Mesh, PartitionSpec as P

beta_one = 0.9
beta_two = 0.999
learn_rate = 0.001
decay_rate = 0.1
epsilon = 1e-08
step_count = 100.0

DP = ("xh", "z", "c")
MP = ("xl", "y")


def adamw(weights, first_moment, second_moment, gradient):
    first_new = beta_one * first_moment + (1.0 - beta_one) * gradient
    second_new = beta_two * second_moment + (1.0 - beta_two) * gradient * gradient
    corrected_first = first_new / (1.0 - beta_one**step_count)
    corrected_second = second_new / (1.0 - beta_two**step_count)
    update = corrected_first / (jnp.sqrt(corrected_second) + epsilon)
    weights_new = weights - learn_rate * (update + decay_rate * weights)
    return (weights_new, first_new, second_new)


def one_hot(index, count):
    rows = lax.broadcasted_iota(jnp.int32, (count, index.shape[0]), 0)
    return (rows == index[None, :]).astype(jnp.bfloat16)


def shift(a, axis, by):
    n = lax.axis_size(axis)
    return lax.ppermute(a, axis, [(i, (i + by) % n) for i in range(n)])


def ring_gather(piece, axis):
    n = lax.axis_size(axis)
    up, down = piece, piece
    got = {0: piece}
    for k in range(1, n // 2):
        up, down = shift(up, axis, 1), shift(down, axis, -1)
        got[n - k], got[k] = up, down
    half = piece.shape[0] // 2
    up, down = shift(up[:half], axis, 1), shift(down[half:], axis, -1)
    got[n // 2] = jnp.concatenate([up, down])
    return [got[k] for k in range(n)]


def add(*terms):
    return sum(t.astype(jnp.float32) for t in terms).astype(terms[0].dtype)


def ring_scatter(part, far_up, far_down, axis, tie):
    n = lax.axis_size(axis)
    h = n // 2
    cut = far_up.shape[2]
    up, down = shift(far_up, axis, 1), shift(far_down, axis, -1)
    up = jnp.concatenate([add(part[h - 1][:, :, :cut], up), part[h - 1][:, :, cut:]], axis=2)
    down = jnp.concatenate([part[h + 1][:, :, :cut], add(part[h + 1][:, :, cut:], down)], axis=2)
    for k in range(h - 1, 0, -1):
        up, down = shift(up, axis, 1), shift(down, axis, -1)
        if k > 1:
            up, down = add(up, part[k - 1]), add(down, part[n - k + 1])
        if k == h - 1:
            up, tie = lax.optimization_barrier((up, tie))
    return add(part[0], up, down), tie


def gradient_parts(order, tiles, outs, n_z):
    n_mp = len(tiles)
    width = tiles[0][0].shape[1]
    rows = sum(t.shape[0] for t in tiles[0]) // n_z
    cols = outs[0].shape[1]
    kind = outs[0].dtype
    flat = [t for tile in tiles for t in tile]
    sizes = [len(tile) for tile in tiles]
    far = n_z // 2

    def body(order_ref, *refs):
        tile_refs, o_refs = list(refs[: len(flat)]), refs[len(flat) : len(flat) + len(outs)]
        g_ref, up_ref, down_ref, t_ref = refs[len(flat) + len(outs) :]
        step = width // len(outs)
        for i in range(n_mp):
            at = order_ref[i]
            k = 0
            for ref in [tile_refs.pop(0) for _ in range(sizes[i])]:
                acc = None
                for j, o_ref in enumerate(o_refs):
                    term = jnp.dot(ref[:, j * step : (j + 1) * step], o_ref[...], preferred_element_type=jnp.float32)
                    acc = term if acc is None else acc + term
                acc = acc.astype(kind)
                for r in range(0, ref.shape[0], rows):
                    piece = acc[r : r + rows]
                    if k == far:
                        up_ref[at] = piece[:, : cols // 2]
                        down_ref[at] = piece[:, cols // 2 :]
                    else:
                        g_ref[k - (k > far), at] = piece
                    t_ref[k, at] = ref[r : r + rows]
                    k += 1

    vmem = pl.BlockSpec(memory_space=pltpu.VMEM)
    g, up, down, tiles_all = pl.pallas_call(
        body,
        out_shape=(
            jax.ShapeDtypeStruct((n_z - 1, n_mp, rows, cols), kind),
            jax.ShapeDtypeStruct((n_mp, rows, cols // 2), kind),
            jax.ShapeDtypeStruct((n_mp, rows, cols // 2), kind),
            jax.ShapeDtypeStruct((n_z, n_mp, rows, width), kind),
        ),
        in_specs=[pl.BlockSpec(memory_space=pltpu.SMEM)] + [vmem] * (len(flat) + len(outs)),
        out_specs=(vmem,) * 4,
        name="gradient_parts",
    )(order, *flat, *outs)
    return {k: g[k - (k > far)] for k in range(n_z) if k != far}, up, down, tiles_all


def local(context, out_grad, master, moment_one, moment_two, new_owner, old_pieces):
    f32, bf16 = jnp.float32, jnp.bfloat16
    n_dp, n_mp, n_z, n_y = lax.axis_size(DP), lax.axis_size(MP), lax.axis_size("z"), lax.axis_size("y")
    d, xh, z, c = lax.axis_index(DP), lax.axis_index("xh"), lax.axis_index("z"), lax.axis_index("c")
    xl, y = lax.axis_index("xl"), lax.axis_index("y")
    blocks, width = master.shape[1:]
    tokens, cols = context.shape
    per_dev = cols // width
    per_row = per_dev * n_mp
    rows = blocks // per_row
    own_slab = new_owner[d]
    positions = (lax.dynamic_index_in_dim(old_pieces, d, 1, keepdims=False) - own_slab * blocks).reshape(-1)
    rel = jnp.arange(n_mp, dtype=jnp.int32)
    mp_of_rel = (rel // n_y ^ xl) * n_y + (rel % n_y + y) % n_y

    states = jnp.concatenate([master[0], moment_one[0], moment_two[0]], axis=1).astype(bf16)
    states = lax.all_to_all(states, DP, 0, 0, tiled=True)

    spot = jnp.arange(cols, dtype=jnp.int32)
    slab = spot // rows
    dp_of = ((slab // (2 * n_z) ^ xh) * n_z + (slab % n_z + z) % n_z) * 2 + (slab // n_z % 2 ^ c)
    hit = dp_of[:, None] == jnp.arange(n_dp, dtype=jnp.int32)[None]
    wanted = jnp.sum(jnp.where(hit, new_owner[None], 0), axis=1, keepdims=True) * rows + (spot % rows)[:, None]
    select = (lax.broadcasted_iota(jnp.int32, (cols, cols), 1) == wanted).astype(bf16)
    ct = lax.dot_general(select, context, (((1,), (1,)), ((), ())), preferred_element_type=f32).astype(bf16)
    half = cols // 2
    quarter = half // 2
    ct_x = shift(ct[half:], "xh", 1)
    ct_a = jnp.concatenate([ct[:quarter], ct_x[:quarter]], axis=1)
    ct_b = shift(jnp.concatenate([ct[quarter:half], ct_x[quarter:]], axis=1), "c", 1)
    og_x = shift(out_grad, "xh", 1)
    og_c, og_xc = shift(out_grad, "c", 1), shift(og_x, "c", 1)

    tile = jnp.concatenate([ct_a, ct_b], axis=1)
    cut = quarter // 2
    tiles = []
    for own in (tile, shift(tile, "xl", 1)):
        up, down = shift(own, "y", 1), shift(own, "y", -1)
        far = [shift(down[:cut], "y", -1), shift(up[cut:], "y", 1)]
        tiles += [[own], [down], far, [up]]

    w_at = (positions % per_row) * rows + positions // per_row
    w_t = jnp.dot(one_hot(w_at, blocks), states[:, :width], preferred_element_type=f32).astype(bf16)
    w_t = lax.all_to_all(w_t.reshape(n_mp, per_dev, rows, width), MP, 0, 0, tiled=True)
    w_t = w_t.transpose(0, 2, 1, 3).reshape(n_mp, rows, cols)
    placed = jnp.dot(one_hot(positions, blocks), states, preferred_element_type=f32)
    grads, far_up, far_down, ct_all = gradient_parts(mp_of_rel, tiles, [out_grad, og_x, og_c, og_xc], n_z)
    w_all = jnp.concatenate(ring_gather(w_t, "z")).reshape(n_z * n_mp * rows, cols)

    grad, placed = ring_scatter(grads, far_up, far_down, "z", placed)
    grad = lax.all_to_all(grad, MP, 0, 0, tiled=True)
    grad = grad.reshape(n_mp, rows, per_dev, width).transpose(1, 0, 2, 3).reshape(blocks, width).astype(f32)

    ct_all = ct_all.reshape(n_z * n_mp * rows, 4 * tokens)
    first = lax.dot_general(ct_all[:, 2 * tokens :], w_all, (((0,), (0,)), ((), ())), preferred_element_type=f32)
    first = shift(first.astype(bf16), "c", 1)
    mine = lax.dot_general(ct_all[:, : 2 * tokens], w_all, (((0,), (0,)), ((), ())), preferred_element_type=f32)
    mine = lax.optimization_barrier(mine)
    partner = shift(add(first[tokens:], mine[tokens:]), "xh", 1)
    proj_out = add(first[:tokens], mine[:tokens], partner)

    weights, first_moment, second_moment = (placed[:, i * width : (i + 1) * width] for i in range(3))
    weights_new, first_new, second_new = adamw(weights, first_moment, second_moment, grad)
    return (proj_out, weights_new[None], first_new[None], second_new[None])


def solution(mesh):
    fine = Mesh(mesh.devices.reshape(2, 8, 2, 2, 4), DP + MP)
    placed = (P(DP, MP), P(DP, MP), P(MP, DP, None), P(MP, DP, None), P(MP, DP, None), P(), P())
    return jax.shard_map(
        local,
        mesh=fine,
        in_specs=placed,
        out_specs=(P(DP, MP), P(MP, DP, None), P(MP, DP, None), P(MP, DP, None)),
        check_vma=False,
    )
```

```python
import jax
import jax.numpy as jnp
from jax import lax
from jax.experimental import pallas as pl
from jax.experimental.pallas import tpu as pltpu
from jax.sharding import Mesh, PartitionSpec as P

beta_one = 0.9
beta_two = 0.999
learn_rate = 0.001
decay_rate = 0.1
epsilon = 1e-08
step_count = 100.0

DP = ("xh", "z", "c")
MP = ("xl", "y")


def adamw(weights, first_moment, second_moment, gradient):
    first_new = beta_one * first_moment + (1.0 - beta_one) * gradient
    second_new = beta_two * second_moment + (1.0 - beta_two) * gradient * gradient
    corrected_first = first_new / (1.0 - beta_one**step_count)
    corrected_second = second_new / (1.0 - beta_two**step_count)
    update = corrected_first / (jnp.sqrt(corrected_second) + epsilon)
    weights_new = weights - learn_rate * (update + decay_rate * weights)
    return (weights_new, first_new, second_new)


def one_hot(index, count):
    rows = lax.broadcasted_iota(jnp.int32, (count, index.shape[0]), 0)
    return (rows == index[None, :]).astype(jnp.bfloat16)


def shift(a, axis, by):
    n = lax.axis_size(axis)
    return lax.ppermute(a, axis, [(i, (i + by) % n) for i in range(n)])


def ring_gather(piece, axis):
    n = lax.axis_size(axis)
    up, down = piece, piece
    got = {0: piece}
    for k in range(1, n // 2):
        up, down = shift(up, axis, 1), shift(down, axis, -1)
        got[n - k], got[k] = up, down
    half = piece.shape[0] // 2
    up, down = shift(up[:half], axis, 1), shift(down[half:], axis, -1)
    got[n // 2] = jnp.concatenate([up, down])
    return [got[k] for k in range(n)]


def add(*terms):
    return sum(t.astype(jnp.float32) for t in terms).astype(terms[0].dtype)


def ring_scatter(part, far_up, far_down, axis):
    n = lax.axis_size(axis)
    h = n // 2
    cut = far_up.shape[2]
    up, down = shift(far_up, axis, 1), shift(far_down, axis, -1)
    up = jnp.concatenate([add(part[h - 1][:, :, :cut], up), part[h - 1][:, :, cut:]], axis=2)
    down = jnp.concatenate([part[h + 1][:, :, :cut], add(part[h + 1][:, :, cut:], down)], axis=2)
    for k in range(h - 1, 0, -1):
        up, down = shift(up, axis, 1), shift(down, axis, -1)
        if k > 1:
            up, down = add(up, part[k - 1]), add(down, part[n - k + 1])
    return add(part[0], up, down)


def gradient_parts(order, tiles, outs, n_z):
    n_mp = len(tiles)
    width = tiles[0][0].shape[1]
    rows = sum(t.shape[0] for t in tiles[0]) // n_z
    cols = outs[0].shape[1]
    kind = outs[0].dtype
    flat = [t for tile in tiles for t in tile]
    sizes = [len(tile) for tile in tiles]
    far = n_z // 2

    def body(order_ref, *refs):
        tile_refs, o_refs = list(refs[: len(flat)]), refs[len(flat) : len(flat) + len(outs)]
        g_ref, up_ref, down_ref, t_ref = refs[len(flat) + len(outs) :]
        step = width // len(outs)
        for i in range(n_mp):
            at = order_ref[i]
            k = 0
            for ref in [tile_refs.pop(0) for _ in range(sizes[i])]:
                acc = None
                for j, o_ref in enumerate(o_refs):
                    term = jnp.dot(ref[:, j * step : (j + 1) * step], o_ref[...], preferred_element_type=jnp.float32)
                    acc = term if acc is None else acc + term
                acc = acc.astype(kind)
                for r in range(0, ref.shape[0], rows):
                    piece = acc[r : r + rows]
                    if k == far:
                        up_ref[at] = piece[:, : cols // 2]
                        down_ref[at] = piece[:, cols // 2 :]
                    else:
                        g_ref[k - (k > far), at] = piece
                    t_ref[k, at] = ref[r : r + rows]
                    k += 1

    vmem = pl.BlockSpec(memory_space=pltpu.VMEM)
    g, up, down, tiles_all = pl.pallas_call(
        body,
        out_shape=(
            jax.ShapeDtypeStruct((n_z - 1, n_mp, rows, cols), kind),
            jax.ShapeDtypeStruct((n_mp, rows, cols // 2), kind),
            jax.ShapeDtypeStruct((n_mp, rows, cols // 2), kind),
            jax.ShapeDtypeStruct((n_z, n_mp, rows, width), kind),
        ),
        in_specs=[pl.BlockSpec(memory_space=pltpu.SMEM)] + [vmem] * (len(flat) + len(outs)),
        out_specs=(vmem,) * 4,
        name="gradient_parts",
    )(order, *flat, *outs)
    return {k: g[k - (k > far)] for k in range(n_z) if k != far}, up, down, tiles_all


def local(context, out_grad, master, moment_one, moment_two, new_owner, old_pieces):
    f32, bf16 = jnp.float32, jnp.bfloat16
    n_dp, n_mp, n_z, n_y = lax.axis_size(DP), lax.axis_size(MP), lax.axis_size("z"), lax.axis_size("y")
    d, xh, z, c = lax.axis_index(DP), lax.axis_index("xh"), lax.axis_index("z"), lax.axis_index("c")
    xl, y = lax.axis_index("xl"), lax.axis_index("y")
    blocks, width = master.shape[1:]
    tokens, cols = context.shape
    per_dev = cols // width
    per_row = per_dev * n_mp
    rows = blocks // per_row
    own_slab = new_owner[d]
    positions = (lax.dynamic_index_in_dim(old_pieces, d, 1, keepdims=False) - own_slab * blocks).reshape(-1)
    rel = jnp.arange(n_mp, dtype=jnp.int32)
    mp_of_rel = (rel // n_y ^ xl) * n_y + (rel % n_y + y) % n_y

    w_in = lax.all_to_all(master[0].astype(bf16), DP, 0, 0, tiled=True)

    spot = jnp.arange(cols, dtype=jnp.int32)
    slab = spot // rows
    dp_of = ((slab // (2 * n_z) ^ xh) * n_z + (slab % n_z + z) % n_z) * 2 + (slab // n_z % 2 ^ c)
    hit = dp_of[:, None] == jnp.arange(n_dp, dtype=jnp.int32)[None]
    wanted = jnp.sum(jnp.where(hit, new_owner[None], 0), axis=1, keepdims=True) * rows + (spot % rows)[:, None]
    select = (lax.broadcasted_iota(jnp.int32, (cols, cols), 1) == wanted).astype(bf16)
    ct = lax.dot_general(select, context, (((1,), (1,)), ((), ())), preferred_element_type=f32).astype(bf16)
    half = cols // 2
    quarter = half // 2
    ct_x = shift(ct[half:], "xh", 1)
    ct_a = jnp.concatenate([ct[:quarter], ct_x[:quarter]], axis=1)
    ct_b = shift(jnp.concatenate([ct[quarter:half], ct_x[quarter:]], axis=1), "c", 1)
    og_x = shift(out_grad, "xh", 1)
    og_c, og_xc = shift(out_grad, "c", 1), shift(og_x, "c", 1)

    tile = jnp.concatenate([ct_a, ct_b], axis=1)
    cut = quarter // 2
    tiles = []
    for own in (tile, shift(tile, "xl", 1)):
        up, down = shift(own, "y", 1), shift(own, "y", -1)
        far = [shift(down[:cut], "y", -1), shift(up[cut:], "y", 1)]
        tiles += [[own], [down], far, [up]]

    w_at = (positions % per_row) * rows + positions // per_row
    w_t = jnp.dot(one_hot(w_at, blocks), w_in, preferred_element_type=f32).astype(bf16)
    w_t = lax.all_to_all(w_t.reshape(n_mp, per_dev, rows, width), MP, 0, 0, tiled=True)
    w_t = w_t.transpose(0, 2, 1, 3).reshape(n_mp, rows, cols)
    moments = jnp.concatenate([moment_one[0], moment_two[0]], axis=1).astype(bf16)
    w_t, moments = lax.optimization_barrier((w_t, moments))
    m_in = lax.all_to_all(moments, DP, 0, 0, tiled=True)
    placed = one_hot(positions, blocks)
    placed = jnp.dot(placed, jnp.concatenate([w_in, m_in], axis=1), preferred_element_type=f32)
    grads, far_up, far_down, ct_all = gradient_parts(mp_of_rel, tiles, [out_grad, og_x, og_c, og_xc], n_z)
    w_all = jnp.concatenate(ring_gather(w_t, "z")).reshape(n_z * n_mp * rows, cols)

    grad = ring_scatter(grads, far_up, far_down, "z")
    grad = lax.all_to_all(grad, MP, 0, 0, tiled=True)
    grad = grad.reshape(n_mp, rows, per_dev, width).transpose(1, 0, 2, 3).reshape(blocks, width).astype(f32)

    ct_all = ct_all.reshape(n_z * n_mp * rows, 4 * tokens)
    first = lax.dot_general(ct_all[:, 2 * tokens :], w_all, (((0,), (0,)), ((), ())), preferred_element_type=f32)
    first = shift(first.astype(bf16), "c", 1)
    mine = lax.dot_general(ct_all[:, : 2 * tokens], w_all, (((0,), (0,)), ((), ())), preferred_element_type=f32)
    mine = lax.optimization_barrier(mine)
    partner = shift(add(first[tokens:], mine[tokens:]), "xh", 1)
    proj_out = add(first[:tokens], mine[:tokens], partner)

    weights, first_moment, second_moment = (placed[:, i * width : (i + 1) * width] for i in range(3))
    weights_new, first_new, second_new = adamw(weights, first_moment, second_moment, grad)
    return (proj_out, weights_new[None], first_new[None], second_new[None])


def solution(mesh):
    fine = Mesh(mesh.devices.reshape(2, 8, 2, 2, 4), DP + MP)
    placed = (P(DP, MP), P(DP, MP), P(MP, DP, None), P(MP, DP, None), P(MP, DP, None), P(), P())
    return jax.shard_map(
        local,
        mesh=fine,
        in_specs=placed,
        out_specs=(P(DP, MP), P(MP, DP, None), P(MP, DP, None), P(MP, DP, None)),
        check_vma=False,
    )
```

```python
import jax
import jax.numpy as jnp
from jax import lax
from jax.experimental import pallas as pl
from jax.experimental.pallas import tpu as pltpu
from jax.sharding import Mesh, PartitionSpec as P

beta_one = 0.9
beta_two = 0.999
learn_rate = 0.001
decay_rate = 0.1
epsilon = 1e-08
step_count = 100.0

DP = ("xh", "z", "c")
MP = ("xl", "y")


def adamw(weights, first_moment, second_moment, gradient):
    first_new = beta_one * first_moment + (1.0 - beta_one) * gradient
    second_new = beta_two * second_moment + (1.0 - beta_two) * gradient * gradient
    corrected_first = first_new / (1.0 - beta_one**step_count)
    corrected_second = second_new / (1.0 - beta_two**step_count)
    update = corrected_first / (jnp.sqrt(corrected_second) + epsilon)
    weights_new = weights - learn_rate * (update + decay_rate * weights)
    return (weights_new, first_new, second_new)


def one_hot(index, count):
    rows = lax.broadcasted_iota(jnp.int32, (count, index.shape[0]), 0)
    return (rows == index[None, :]).astype(jnp.bfloat16)


def shift(a, axis, by):
    n = lax.axis_size(axis)
    return lax.ppermute(a, axis, [(i, (i + by) % n) for i in range(n)])


def ring_gather(piece, axis):
    n = lax.axis_size(axis)
    up, down = piece, piece
    got = {0: piece}
    for k in range(1, n // 2):
        up, down = shift(up, axis, 1), shift(down, axis, -1)
        got[n - k], got[k] = up, down
    half = piece.shape[0] // 2
    up, down = shift(up[:half], axis, 1), shift(down[half:], axis, -1)
    got[n // 2] = jnp.concatenate([up, down])
    return [got[k] for k in range(n)]


def add(*terms):
    return sum(t.astype(jnp.float32) for t in terms).astype(terms[0].dtype)


def ring_scatter(part, far_up, far_down, axis):
    n = lax.axis_size(axis)
    h = n // 2
    cut = far_up.shape[2]
    up, down = shift(far_up, axis, 1), shift(far_down, axis, -1)
    up = jnp.concatenate([add(part[h - 1][:, :, :cut], up), part[h - 1][:, :, cut:]], axis=2)
    down = jnp.concatenate([part[h + 1][:, :, :cut], add(part[h + 1][:, :, cut:], down)], axis=2)
    for k in range(h - 1, 0, -1):
        up, down = shift(up, axis, 1), shift(down, axis, -1)
        if k > 1:
            up, down = add(up, part[k - 1]), add(down, part[n - k + 1])
    return add(part[0], up, down)


def gradient_parts(order, tiles, outs, n_z):
    n_mp = len(tiles)
    width = tiles[0][0].shape[1]
    rows = sum(t.shape[0] for t in tiles[0]) // n_z
    cols = outs[0].shape[1]
    kind = outs[0].dtype
    flat = [t for tile in tiles for t in tile]
    sizes = [len(tile) for tile in tiles]
    far = n_z // 2

    def body(order_ref, *refs):
        tile_refs, o_refs = list(refs[: len(flat)]), refs[len(flat) : len(flat) + len(outs)]
        g_ref, up_ref, down_ref, t_ref, o_all, t_all = refs[len(flat) + len(outs) :]
        step = width // len(outs)
        for j, o_ref in enumerate(o_refs):
            o_all[j * step : (j + 1) * step] = o_ref[...]
        depth = n_z * rows
        at = 0
        for ref in tile_refs:
            t_all[at : at + ref.shape[0]] = ref[...]
            at += ref.shape[0]
        for side in range(2):
            lanes = slice(side * cols // 2, (side + 1) * cols // 2)
            acc = jnp.dot(t_all[...], o_all[:, lanes], preferred_element_type=jnp.float32)
            for i in range(n_mp):
                to = order_ref[i]
                for k in range(n_z):
                    at = i * depth + k * rows
                    piece = acc[at : at + rows].astype(kind)
                    if k == far:
                        (down_ref if side else up_ref)[to] = piece
                    else:
                        g_ref[k - (k > far), to, :, lanes] = piece
                    if side == 0:
                        t_ref[k, to] = t_all[at : at + rows]

    vmem = pl.BlockSpec(memory_space=pltpu.VMEM)
    g, up, down, tiles_all = pl.pallas_call(
        body,
        out_shape=(
            jax.ShapeDtypeStruct((n_z - 1, n_mp, rows, cols), kind),
            jax.ShapeDtypeStruct((n_mp, rows, cols // 2), kind),
            jax.ShapeDtypeStruct((n_mp, rows, cols // 2), kind),
            jax.ShapeDtypeStruct((n_z, n_mp, rows, width), kind),
        ),
        in_specs=[pl.BlockSpec(memory_space=pltpu.SMEM)] + [vmem] * (len(flat) + len(outs)),
        out_specs=(vmem,) * 4,
        scratch_shapes=[pltpu.VMEM((width, cols), kind), pltpu.VMEM((n_mp * n_z * rows, width), kind)],
        name="gradient_parts",
    )(order, *flat, *outs)
    return {k: g[k - (k > far)] for k in range(n_z) if k != far}, up, down, tiles_all


def local(context, out_grad, master, moment_one, moment_two, new_owner, old_pieces):
    f32, bf16 = jnp.float32, jnp.bfloat16
    n_dp, n_mp, n_z, n_y = lax.axis_size(DP), lax.axis_size(MP), lax.axis_size("z"), lax.axis_size("y")
    d, xh, z, c = lax.axis_index(DP), lax.axis_index("xh"), lax.axis_index("z"), lax.axis_index("c")
    xl, y = lax.axis_index("xl"), lax.axis_index("y")
    blocks, width = master.shape[1:]
    tokens, cols = context.shape
    per_dev = cols // width
    per_row = per_dev * n_mp
    rows = blocks // per_row
    own_slab = new_owner[d]
    positions = (lax.dynamic_index_in_dim(old_pieces, d, 1, keepdims=False) - own_slab * blocks).reshape(-1)
    rel = jnp.arange(n_mp, dtype=jnp.int32)
    mp_of_rel = (rel // n_y ^ xl) * n_y + (rel % n_y + y) % n_y

    w_in = lax.all_to_all(master[0].astype(bf16), DP, 0, 0, tiled=True)

    spot = jnp.arange(cols, dtype=jnp.int32)
    slab = spot // rows
    dp_of = ((slab // (2 * n_z) ^ xh) * n_z + (slab % n_z + z) % n_z) * 2 + (slab // n_z % 2 ^ c)
    hit = dp_of[:, None] == jnp.arange(n_dp, dtype=jnp.int32)[None]
    wanted = jnp.sum(jnp.where(hit, new_owner[None], 0), axis=1, keepdims=True) * rows + (spot % rows)[:, None]
    select = (lax.broadcasted_iota(jnp.int32, (cols, cols), 1) == wanted).astype(bf16)
    ct = lax.dot_general(select, context, (((1,), (1,)), ((), ())), preferred_element_type=f32).astype(bf16)
    half = cols // 2
    quarter = half // 2
    ct_x = shift(ct[half:], "xh", 1)
    ct_a = jnp.concatenate([ct[:quarter], ct_x[:quarter]], axis=1)
    ct_b = shift(jnp.concatenate([ct[quarter:half], ct_x[quarter:]], axis=1), "c", 1)
    og_x = shift(out_grad, "xh", 1)
    og_c, og_xc = shift(out_grad, "c", 1), shift(og_x, "c", 1)

    tile = jnp.concatenate([ct_a, ct_b], axis=1)
    cut = quarter // 2
    tiles = []
    for own in (tile, shift(tile, "xl", 1)):
        up, down = shift(own, "y", 1), shift(own, "y", -1)
        far = [shift(down[:cut], "y", -1), shift(up[cut:], "y", 1)]
        tiles += [[own], [down], far, [up]]

    w_at = (positions % per_row) * rows + positions // per_row
    w_t = jnp.dot(one_hot(w_at, blocks), w_in, preferred_element_type=f32).astype(bf16)
    w_t = lax.all_to_all(w_t.reshape(n_mp, per_dev, rows, width), MP, 0, 0, tiled=True)
    w_t = w_t.transpose(0, 2, 1, 3).reshape(n_mp, rows, cols)
    moments = jnp.concatenate([moment_one[0], moment_two[0]], axis=1).astype(bf16)
    w_t, moments = lax.optimization_barrier((w_t, moments))
    m_in = lax.all_to_all(moments, DP, 0, 0, tiled=True)
    placed = one_hot(positions, blocks)
    placed = jnp.dot(placed, jnp.concatenate([w_in, m_in], axis=1), preferred_element_type=f32)
    grads, far_up, far_down, ct_all = gradient_parts(mp_of_rel, tiles, [out_grad, og_x, og_c, og_xc], n_z)
    w_all = jnp.concatenate(ring_gather(w_t, "z")).reshape(n_z * n_mp * rows, cols)

    grad = ring_scatter(grads, far_up, far_down, "z")
    grad = lax.all_to_all(grad, MP, 0, 0, tiled=True)
    grad = grad.reshape(n_mp, rows, per_dev, width).transpose(1, 0, 2, 3).reshape(blocks, width).astype(f32)

    ct_all = ct_all.reshape(n_z * n_mp * rows, 4 * tokens)
    first = lax.dot_general(ct_all[:, 2 * tokens :], w_all, (((0,), (0,)), ((), ())), preferred_element_type=f32)
    first = shift(first.astype(bf16), "c", 1)
    mine = lax.dot_general(ct_all[:, : 2 * tokens], w_all, (((0,), (0,)), ((), ())), preferred_element_type=f32)
    mine = lax.optimization_barrier(mine)
    partner = shift(add(first[tokens:], mine[tokens:]), "xh", 1)
    proj_out = add(first[:tokens], mine[:tokens], partner)

    weights, first_moment, second_moment = (placed[:, i * width : (i + 1) * width] for i in range(3))
    weights_new, first_new, second_new = adamw(weights, first_moment, second_moment, grad)
    return (proj_out, weights_new[None], first_new[None], second_new[None])


def solution(mesh):
    fine = Mesh(mesh.devices.reshape(2, 8, 2, 2, 4), DP + MP)
    placed = (P(DP, MP), P(DP, MP), P(MP, DP, None), P(MP, DP, None), P(MP, DP, None), P(), P())
    return jax.shard_map(
        local,
        mesh=fine,
        in_specs=placed,
        out_specs=(P(DP, MP), P(MP, DP, None), P(MP, DP, None), P(MP, DP, None)),
        check_vma=False,
    )
```
